256 devices in a mesh: region: 16 (over z, core), tracer: 16 (over y, x).
Axes of the slice: x: 4, y: 4, z: 8, core: 2. Of those that a mesh axis runs over, the one named last changes fastest.
Arguments:
- concentration: float32 [40, 128, 32768], P(None, 'tracer', 'region'), may hold values from 0 to 1
- courant: float32 [2, 3, 40, 32768], P(None, None, None, ('region', 'tracer')), may hold values from -0.3 to 0.3
- diffusivity: float32 [2, 39, 32768], P(None, None, ('region', 'tracer')), may hold values from 0.2 to 5
- release_rate: float32 [40, 128], P(None, 'tracer'), may hold values from 0.2 to 2
- release_cell: int32 [128], P('tracer'), may hold values from 0 to 32767
- neighbour: int32 [3, 32768], P(None, 'region'), may hold values from -1 to 2559, as said below
- send_rows: int32 [16, 16, 32], P('region'), may hold values from -1 to 63, as said below
Outputs:
- final_field: float32 [40, 128, 32768], P(None, 'tracer', 'region')
The draws below stay inside these ranges and needn't reach their ends.
Inputs may be any that keep to these rules, and one draw needn't show every extreme that they name: `neighbour`: A value n below 2048 is a triangle of the same region; n of 2048 or more names halo slot n - 2048, slot s of the list from region p being p * 32 + s, and only live slots are named; -1 is a closed face. send_rows[p, r, s] is the rim row (triangle 2048 - 64 + row of region p) that region p sends to region r in slot s; -1 marks an empty slot and live slots come first; rows of one list differ; a region sends nothing to itself; every region fills all 32 slots to one peer and receives a full list from one peer.
All inputs are finite; a program needn't handle non-finite values.
Results may differ from the reference program's by a relative error of at most 0.0001.
Values sent between devices are 32-bit elements; how exact they have to be, the bound alone decides.
No kernel may reach another device: no remote copies, remote signals or barrier semaphores. Data moves between devices by JAX's collectives and lax.ppermute only.
A program may use at most 128 MiB of HBM per device.

```python
import math
import jax
import jax.numpy as jnp

LAYERS = 40
CELL_DEV = 2048
SEND_CAP = 32
HOURS = 2
STEPS = 6
BOUND = 64
REGIONS = 16
CELLS = 32768
TRACERS = 128


def cycle_counts(key):
    base = jax.random.fold_in(key, 11)
    keys = jax.random.split(base, 3)
    cycle_order = jax.random.permutation(keys[0], REGIONS).astype(jnp.int32)
    cycle_place = jnp.zeros((REGIONS,), jnp.int32).at[cycle_order].set(jnp.arange(REGIONS, dtype=jnp.int32))
    cycle_gap = (cycle_place[None, :] - cycle_place[:, None]) % REGIONS
    distance = jnp.maximum(jnp.minimum(cycle_gap, REGIONS - cycle_gap), 1)
    far_count = jax.random.randint(keys[1], (REGIONS, REGIONS), 1, 1 + jnp.maximum(SEND_CAP // distance, 1))
    back_count = jax.random.randint(keys[2], (REGIONS, REGIONS), SEND_CAP // 2, SEND_CAP + 1)
    counts = jnp.where(cycle_gap == REGIONS - 1, back_count, far_count)
    counts = jnp.where(cycle_gap == 1, SEND_CAP, counts)
    counts = jnp.where(cycle_gap == 0, 0, counts)
    return counts.astype(jnp.int32)


def draw_send_rows(key, part):
    counts = cycle_counts(key)
    scores = jax.random.randint(jax.random.fold_in(key, 12), (REGIONS, REGIONS, BOUND), 0, 1 << 20) * BOUND
    scores = scores + jnp.arange(BOUND, dtype=jnp.int32)[None, None, :]
    full_peer = jnp.argmax((counts[0] == SEND_CAP).astype(jnp.int32)).astype(jnp.int32)
    region_id = jnp.arange(REGIONS, dtype=jnp.int32)
    row_id = jnp.arange(BOUND, dtype=jnp.int32)
    forced = (region_id[:, None, None] == 0) & (region_id[None, :, None] == full_peer) & (row_id[None, None, :] == BOUND - 1)
    scores = jnp.where(forced, -1, scores)
    shuffled = jnp.argsort(scores, axis=-1)[:, :, :SEND_CAP].astype(jnp.int32)
    slot_id = jnp.arange(SEND_CAP, dtype=jnp.int32)
    return jnp.where(slot_id[None, None, :] < counts[:, :, None], shuffled, -1).astype(jnp.int32)


def draw_neighbour(key, part):
    counts = cycle_counts(key)
    global_cell = jnp.arange(CELLS, dtype=jnp.int32)[None, :]
    face = jnp.arange(3, dtype=jnp.int32)[:, None]
    owner = global_cell // CELL_DEV
    local_id = global_cell % CELL_DEV
    face_slot = (CELL_DEV - 1 - local_id) * 3 + face
    source = jnp.minimum(face_slot // SEND_CAP, REGIONS - 1)
    slot_id = face_slot % SEND_CAP
    is_live = (face_slot < REGIONS * SEND_CAP) & (slot_id < counts[source, owner])
    keys = jax.random.split(jax.random.fold_in(key, 13), 3)
    offset = jax.random.randint(keys[0], (3, CELLS), 1, 33) * (2 * jax.random.randint(keys[1], (3, CELLS), 0, 2) - 1)
    local_cell = (local_id + offset) % CELL_DEV
    is_coast = jax.random.randint(keys[2], (3, CELLS), 0, 16) == 0
    return jnp.where(is_live, CELL_DEV + face_slot, jnp.where(is_coast, -1, local_cell)).astype(jnp.int32)


def set_ends(values, rng, smallest, high):
    index_at = [jax.random.randint(jax.random.fold_in(rng, axis), (), 0, length) for axis, length in enumerate(values.shape)]
    main_axis = values.shape.index(max(values.shape))
    next_to = index_at[:main_axis] + [(index_at[main_axis] + 1) % values.shape[main_axis]] + index_at[main_axis + 1:]
    return values.at[tuple(index_at)].set(smallest).at[tuple(next_to)].set(high)


def block_scale(key, dims, shards, least, high):
    def one(axis_at, shards_of):
        heights = jax.random.uniform(jax.random.fold_in(jax.random.fold_in(key, 6), axis_at), (shards_of,), jnp.float32, least / len(shards), high / len(shards))
        return jnp.repeat(jnp.exp(heights), dims[axis_at] // shards_of).reshape((-1,) + (1,) * (len(dims) - axis_at - 1))

    loudness = one(*shards[0])
    for cut in shards[1:]:
        loudness = loudness * one(*cut)
    return loudness


def setup_inputs(seed: int = 0) -> dict:
    streams_of = jax.random.split(jax.random.key(seed), 8)
    concentration = jnp.clip(1.0 * jax.random.uniform(streams_of[0], (LAYERS, TRACERS, CELLS), jnp.float32) ** block_scale(streams_of[0], (LAYERS, TRACERS, CELLS), ((1, 16), (2, 16)), -0.2, 0.2), 0.0, 1.0)
    courant = jnp.clip(jax.random.uniform(streams_of[1], (HOURS, 3, LAYERS, CELLS), jnp.float32, -0.3, 0.3) * block_scale(streams_of[1], (HOURS, 3, LAYERS, CELLS), ((3, 256),), -0.4, 0.0), -0.3, 0.3)
    diffusivity = jnp.clip(jnp.exp(math.log(5.0) - 3.218876 * jax.random.uniform(streams_of[2], (HOURS, LAYERS - 1, CELLS), jnp.float32) ** block_scale(streams_of[2], (HOURS, LAYERS - 1, CELLS), ((2, 256),), -0.2, 0.2)), 0.2, 5.0)
    release_rate = jnp.clip(jnp.exp(math.log(2.0) - 2.3025851 * jax.random.uniform(streams_of[3], (LAYERS, TRACERS), jnp.float32) ** block_scale(streams_of[3], (LAYERS, TRACERS), ((1, 16),), -0.2, 0.2)), 0.2, 2.0)
    release_cell = set_ends(jax.random.randint(streams_of[4], (TRACERS,), 0, CELLS), jax.random.fold_in(streams_of[4], 1), 0, CELLS - 1).astype(jnp.int32)
    neighbour = draw_neighbour(jax.random.fold_in(streams_of[7], 71), 0)
    send_rows = draw_send_rows(jax.random.fold_in(streams_of[7], 71), 0)
    return {"concentration": concentration, "courant": courant, "diffusivity": diffusivity, "release_rate": release_rate, "release_cell": release_cell, "neighbour": neighbour, "send_rows": send_rows}


def thomas_solve(mixing, source_term):
    layer_count = source_term.shape[0]
    ratios = []
    partial_value = []
    for layer_index in range(layer_count):
        lower_coef = mixing[layer_index - 1] if layer_index > 0 else jnp.zeros_like(mixing[0])
        upper_coef = mixing[layer_index] if layer_index < layer_count - 1 else jnp.zeros_like(mixing[0])
        pivots = 1.0 + lower_coef + upper_coef
        if layer_index > 0:
            pivots = pivots - lower_coef * ratios[layer_index - 1]
            current = (source_term[layer_index] + lower_coef[None, :] * partial_value[layer_index - 1]) / pivots[None, :]
        else:
            current = source_term[layer_index] / pivots[None, :]
        ratios.append(upper_coef / pivots)
        partial_value.append(current)
    solved = [None] * layer_count
    solved[layer_count - 1] = partial_value[layer_count - 1]
    for layer_index in range(layer_count - 2, -1, -1):
        solved[layer_index] = partial_value[layer_index] + ratios[layer_index][None, :] * solved[layer_index + 1]
    return jnp.stack(solved)


def reference(concentration, courant, diffusivity, release_rate, release_cell, neighbour, send_rows):
    global_cell = jnp.arange(CELLS, dtype=jnp.int32)
    owner = global_cell // CELL_DEV
    halo_slot = jnp.maximum(neighbour - CELL_DEV, 0)
    source = halo_slot // SEND_CAP
    slot_id = halo_slot % SEND_CAP
    rim_row = send_rows[source, owner[None, :], slot_id]
    halo_cell = source * CELL_DEV + CELL_DEV - BOUND + jnp.maximum(rim_row, 0)
    local_cell = owner[None, :] * CELL_DEV + jnp.maximum(neighbour, 0)
    edge_index = jnp.where(neighbour >= CELL_DEV, halo_cell, local_cell).astype(jnp.int32)
    has_edge = neighbour >= 0
    release_mask = (global_cell[None, :] == release_cell[:, None]).astype(jnp.float32)
    field = concentration
    per_hour = STEPS // HOURS
    for step_index in range(STEPS):
        hour_index = step_index // per_hour
        updated = field
        for face in range(3):
            edge_value = jnp.where(has_edge[face][None, None, :], field[:, :, edge_index[face]], jnp.float32(0.0))
            flux_now = courant[hour_index, face][:, None, :]
            updated = updated - (jnp.maximum(flux_now, 0.0) * field + jnp.minimum(flux_now, 0.0) * edge_value)
        updated = updated + release_rate[:, :, None] * release_mask[None, :, :]
        field = thomas_solve(diffusivity[hour_index], updated)
    return field
```

```python
import functools
import jax
import jax.numpy as jnp
from jax import lax
from jax.experimental import pallas as pl
from jax.experimental.pallas import tpu as pltpu
from jax.sharding import PartitionSpec as P

HOURS = 2
STEPS = 6
LANES = 128
SMEM = pltpu.MemorySpace.SMEM
VMEM = pltpu.MemorySpace.VMEM

OWN, EDGE, CARRY, RATIO, INV = 0, 1, 4, 5, 6
KINDS = 7


def pick_lanes(values, lanes):
    return jnp.take_along_axis(values, lanes, axis=1, mode="promise_in_bounds")


def send_pieces(send_ref, lanes_ref, load, layers, peers):
    part = lax.broadcasted_iota(jnp.int32, (8, LANES), 1) // 32
    inside = [part == j for j in range(1, 4)]

    def one(r, carry):
        lanes = lanes_ref[r]
        for g in range(layers // 4):
            piece = pick_lanes(load(4 * g), lanes)
            for j in range(1, 4):
                piece = jnp.where(inside[j - 1], pick_lanes(load(4 * g + j), lanes), piece)
            send_ref[r, g] = piece
        return carry

    lax.fori_loop(0, peers, one, 0)


def pack_kernel(rim_ref, lanes_ref, send_ref):
    send_pieces(send_ref, lanes_ref, lambda l: rim_ref[l], rim_ref.shape[0], send_ref.shape[0])


def prepare_kernel(panel_ref, coef_ref):
    blocks, layers = coef_ref.shape[0], coef_ref.shape[2]
    mix = 3 * layers
    zero = jnp.zeros((1, LANES), jnp.float32)
    for start in range(0, blocks, 8):
        group = range(start, start + 8)
        ratio = {b: zero for b in group}
        lower = {b: zero for b in group}
        for l in range(layers):
            for b in group:
                upper = panel_ref[b, mix + l : mix + l + 1, :]
                pivot = 1.0 + lower[b] + upper - lower[b] * ratio[b]
                inverse = 1.0 / pivot
                coef_ref[b, INV, l : l + 1, :] = inverse
                coef_ref[b, CARRY, l : l + 1, :] = lower[b] * inverse
                ratio[b] = upper * inverse
                lower[b] = upper

    def fill(b, carry):
        inverse = coef_ref[b, INV]
        coef_ref[b, RATIO] = panel_ref[b, mix : mix + layers, :] * inverse
        outflow = jnp.zeros((layers, LANES), jnp.float32)
        for f in range(3):
            flux = panel_ref[b, f * layers : (f + 1) * layers, :]
            outflow = outflow + jnp.maximum(flux, 0.0)
            coef_ref[b, EDGE + f] = -jnp.minimum(flux, 0.0) * inverse
        coef_ref[b, OWN] = (1.0 - outflow) * inverse
        return carry

    lax.fori_loop(0, blocks, fill, 0)


def row(coef_ref, c, kind, l):
    return coef_ref[c, kind, pl.ds(l, 8, stride=0), :]


def advect_block(plan_ref, field_ref, halo_ref, coef_ref, near_ref, rate_ref, acc_ref, i, b, c, n):
    layers = field_ref.shape[0]
    local_blocks = field_ref.shape[2] // LANES
    width = plan_ref.shape[1]
    for l in range(layers):
        acc_ref[i, l] = jnp.zeros((8, LANES), jnp.float32)

    @pl.when(plan_ref[b, width - 1] > 0)
    def _():
        cell = b * LANES + lax.broadcasted_iota(jnp.int32, (8, LANES), 1)
        here = near_ref[n, 3] == cell
        for l in range(layers):
            acc_ref[i, l] = jnp.where(here, rate_ref[l], 0.0) * row(coef_ref, c, INV, l)

    def add_from(source_ref, first):
        def one(k, carry):
            s = plan_ref[b, k]
            place = pl.ds(pl.multiple_of((s - first) * LANES, LANES), LANES)
            lanes = [near_ref[n, f] & (LANES - 1) for f in range(3)]
            inside = [(near_ref[n, f] >> 7) == s for f in range(3)]
            for l in range(layers):
                values = source_ref[l, :, place]
                total = acc_ref[i, l]
                for f in range(3):
                    edge = jnp.where(inside[f], pick_lanes(values, lanes[f]), 0.0)
                    total = total + row(coef_ref, c, EDGE + f, l) * edge
                acc_ref[i, l] = total
            return carry

        return one

    local_count, all_count = plan_ref[b, width - 3], plan_ref[b, width - 2]
    lax.fori_loop(0, local_count, add_from(field_ref, 0), 0)
    lax.fori_loop(local_count, all_count, add_from(halo_ref, local_blocks), 0)


def solve_blocks(field_ref, coef_ref, acc_ref, out_ref, where, where_coef, where_out):
    layers = field_ref.shape[0]
    places = [pl.ds(pl.multiple_of(b * LANES, LANES), LANES) for b in where]
    outs = [pl.ds(pl.multiple_of(b * LANES, LANES), LANES) for b in where_out]
    part = [None] * len(where)
    for l in range(layers):
        for i, place in enumerate(places):
            c = where_coef[i]
            now = row(coef_ref, c, OWN, l) * field_ref[l, :, place] + acc_ref[i, l]
            if l > 0:
                now = now + row(coef_ref, c, CARRY, l) * part[i]
            part[i] = now
            if l < layers - 1:
                acc_ref[i, l] = now
            else:
                out_ref[l, :, outs[i]] = now
    for l in range(layers - 2, -1, -1):
        for i in range(len(places)):
            part[i] = acc_ref[i, l] + row(coef_ref, where_coef[i], RATIO, l) * part[i]
            out_ref[l, :, outs[i]] = part[i]


def rim_kernel(
    last, plan_ref, field_ref, received_ref, coef_ref, near_ref, rate_ref, lanes_ref, *refs
):
    if last:
        halo_ref, new_ref, acc_ref = refs
    else:
        send_ref, halo_ref, new_ref, acc_ref = refs
    layers = field_ref.shape[0]
    block = field_ref.shape[2] // LANES - 1
    lane = lax.broadcasted_iota(jnp.int32, (8, LANES), 1)
    part, slot = lane // 32, lane % 32
    inside = [part == k for k in range(1, 4)]
    moved = [slot + 32 * j for j in range(4)]
    quads = received_ref.shape[0] // 4

    def unpack(g, carry):
        for q in range(quads):
            pieces = [received_ref[4 * q + k, g] for k in range(4)]
            for j in range(4):
                value = pick_lanes(pieces[0], moved[j])
                for k in range(1, 4):
                    value = jnp.where(inside[k - 1], pick_lanes(pieces[k], moved[j]), value)
                halo_ref[4 * g + j, :, q * LANES : (q + 1) * LANES] = value
        return carry

    lax.fori_loop(0, layers // 4, unpack, 0)
    advect_block(
        plan_ref, field_ref, halo_ref, coef_ref, near_ref, rate_ref, acc_ref, 0, block, 0, 0
    )
    solve_blocks(field_ref, coef_ref, acc_ref, new_ref, [block], [0], [0])
    if not last:
        send_pieces(send_ref, lanes_ref, lambda l: new_ref[l], layers, send_ref.shape[0])


GROUP = 5


def bulk_kernel(
    plan_ref, field_ref, halo_ref, rim_ref, coef_ref, near_ref, rate_ref, out_ref, acc_ref
):
    blocks = field_ref.shape[2] // LANES

    def group(g, carry):
        def advect(i, inner):
            b = g * GROUP + i
            advect_block(
                plan_ref, field_ref, halo_ref, coef_ref, near_ref, rate_ref, acc_ref, i, b, b, b
            )
            return inner

        lax.fori_loop(0, GROUP, advect, 0)
        where = [g * GROUP + i for i in range(GROUP)]
        solve_blocks(field_ref, coef_ref, acc_ref, out_ref, where, where, where)
        return carry

    lax.fori_loop(0, (blocks - 1) // GROUP, group, 0)
    out_ref[:, :, (blocks - 1) * LANES :] = rim_ref[...]


def share(value, axis):
    copies = jnp.broadcast_to(value, (lax.axis_size(axis), *value.shape))
    return lax.all_to_all(copies, axis, 0, 0, tiled=True)


def on_device(
    concentration, courant, diffusivity, release_rate, release_cell, neighbour, send_rows
):
    layers, tracers, cells = concentration.shape
    blocks = cells // LANES
    peers, slots = send_rows.shape[1], send_rows.shape[2]
    halo_cells = peers * slots
    rim = 64
    f32 = jnp.float32
    full = pl.BlockSpec(memory_space=VMEM)
    scalars = pl.BlockSpec(memory_space=SMEM)
    message = jax.ShapeDtypeStruct((peers, layers // 4, tracers, LANES), f32)

    def params(mib):
        return pltpu.CompilerParams(vmem_limit_bytes=mib << 20)

    def panel(h):
        empty = jnp.zeros((1, LANES), f32)
        rows = jnp.concatenate([courant[h].reshape(-1, LANES), diffusivity[h], empty], 0)
        return rows

    rows = LANES - rim + jnp.maximum(send_rows[0], 0)
    lanes = jnp.broadcast_to(jnp.tile(rows, (1, LANES // slots))[:, None, :], (peers, 8, LANES))

    send = pl.pallas_call(
        pack_kernel,
        out_shape=message,
        grid=(1,),
        in_specs=[
            pl.BlockSpec((layers, tracers, LANES), lambda i: (0, 0, blocks - 1)),
            pl.BlockSpec((peers, 8, LANES), lambda i: (0, 0, 0)),
        ],
        out_specs=pl.BlockSpec(message.shape, lambda i: (0, 0, 0, 0)),
        name="pack",
    )(concentration, lanes)
    received = lax.all_to_all(send, "region", 0, 0, tiled=True)
    tables = [share(panel(0), "tracer"), None]

    sources = blocks + halo_cells // LANES
    of_block = neighbour.reshape(3, blocks, LANES)
    source_id = jnp.arange(sources, dtype=jnp.int32)
    needed = jnp.any((of_block[..., None] >> 7) == source_id, axis=(0, 2))
    rank = jnp.sum(
        needed[:, None, :] & (source_id[None, None, :] < source_id[None, :, None]), axis=2
    )
    listed = jnp.sum(
        jnp.where(
            needed[:, None, :] & (rank[:, None, :] == source_id[None, :, None]),
            source_id[None, None, :],
            0,
        ),
        axis=2,
    )
    home = release_cell - lax.axis_index("region") * cells
    released = jnp.any(
        (home[None, :] >> 7) == jnp.arange(blocks, dtype=jnp.int32)[:, None], axis=1
    )
    plan = jnp.concatenate(
        [
            listed,
            jnp.sum(needed[:, :blocks], axis=1)[:, None],
            jnp.sum(needed, axis=1)[:, None],
            released[:, None],
        ],
        axis=1,
    ).astype(jnp.int32)
    near = jnp.concatenate(
        [
            jnp.broadcast_to(jnp.moveaxis(of_block, 1, 0)[:, :, None, :], (blocks, 3, 8, LANES)),
            jnp.broadcast_to(home[None, None, :, None], (blocks, 1, 8, LANES)),
        ],
        axis=1,
    )
    rate = jnp.broadcast_to(release_rate[:, :, None], (layers, tracers, LANES))

    coef_shape = (blocks, KINDS, layers, LANES)

    def prepare(table):
        return pl.pallas_call(
            prepare_kernel,
            out_shape=jax.ShapeDtypeStruct(coef_shape, f32),
            in_specs=[full],
            out_specs=full,
            compiler_params=params(32),
            name="prepare",
        )(table)

    new_block = jax.ShapeDtypeStruct((layers, tracers, LANES), f32)
    halo_shape = jax.ShapeDtypeStruct((layers, tracers, halo_cells), f32)

    def whole(shape):
        return pl.BlockSpec(shape, lambda i, n=len(shape): (0,) * n)

    def rim_step(field, received, coef, last):
        outs = (halo_shape, new_block) if last else (message, halo_shape, new_block)
        result = pl.pallas_call(
            functools.partial(rim_kernel, last),
            out_shape=outs,
            grid=(1,),
            in_specs=[
                scalars,
                whole(field.shape),
                whole(received.shape),
                pl.BlockSpec((1, *coef_shape[1:]), lambda i: (blocks - 1, 0, 0, 0)),
                pl.BlockSpec((1, 4, 8, LANES), lambda i: (blocks - 1, 0, 0, 0)),
                whole(rate.shape),
                whole(lanes.shape),
            ],
            out_specs=tuple(whole(o.shape) for o in outs),
            scratch_shapes=[pltpu.VMEM((1, layers, tracers, LANES), f32)],
            compiler_params=params(32),
            name="rim",
        )(plan, field, received, coef, near, rate, lanes)
        return result if not last else (None, *result)

    def bulk_step(field, halo, new, coef):
        return pl.pallas_call(
            bulk_kernel,
            out_shape=jax.ShapeDtypeStruct(field.shape, f32),
            in_specs=[scalars] + [full] * 6,
            out_specs=full,
            scratch_shapes=[pltpu.VMEM((GROUP, layers, tracers, LANES), f32)],
            compiler_params=params(32),
            name="bulk",
        )(plan, field, halo, new, coef, near, rate)

    field = concentration
    per_hour = STEPS // HOURS
    coef = None
    for step in range(STEPS):
        h = step // per_hour
        if step % per_hour == 0:
            coef = prepare(tables[h])
        last = step == STEPS - 1
        send, halo, new = rim_step(field, received, coef, last)
        if step == 0:
            later = panel(1)
            later, _ = lax.optimization_barrier((later, new))
            tables[1] = share(later, "tracer")
        if not last:
            received = lax.all_to_all(send, "region", 0, 0, tiled=True)
        field = bulk_step(field, halo, new, coef)
    return field


def solution(mesh):
    both = ("region", "tracer")
    return jax.shard_map(
        on_device,
        mesh=mesh,
        in_specs=(
            P(None, "tracer", "region"),
            P(None, None, None, both),
            P(None, None, both),
            P(None, "tracer"),
            P("tracer"),
            P(None, "region"),
            P("region", None, None),
        ),
        out_specs=P(None, "tracer", "region"),
        check_vma=False,
    )
```

```python
import functools
import jax
import jax.numpy as jnp
from jax import lax
from jax.experimental import pallas as pl
from jax.experimental.pallas import tpu as pltpu
from jax.sharding import PartitionSpec as P

HOURS = 2
STEPS = 6
LANES = 128
SMEM = pltpu.MemorySpace.SMEM
VMEM = pltpu.MemorySpace.VMEM

OWN, EDGE, CARRY, RATIO, INV = 0, 1, 4, 5, 6
KINDS = 7


def pick_lanes(values, lanes):
    return jnp.take_along_axis(values, lanes, axis=1, mode="promise_in_bounds")


def turn_quarters(values):
    lane = lax.broadcasted_iota(jnp.int32, (8, LANES), 1)
    low = lane < 64
    even = (lane & 32) == 0
    a, b, c, d = values
    a, c = jnp.where(low, a, pltpu.roll(c, 64, 1)), jnp.where(low, pltpu.roll(a, 64, 1), c)
    b, d = jnp.where(low, b, pltpu.roll(d, 64, 1)), jnp.where(low, pltpu.roll(b, 64, 1), d)
    a, b = jnp.where(even, a, pltpu.roll(b, 32, 1)), jnp.where(even, pltpu.roll(a, 96, 1), b)
    c, d = jnp.where(even, c, pltpu.roll(d, 32, 1)), jnp.where(even, pltpu.roll(c, 96, 1), d)
    return a, b, c, d


def send_pieces(send_ref, lanes_ref, load, layers, q):
    lanes = lanes_ref[q]
    for g in range(layers // 4):
        picked = [pick_lanes(load(4 * g + j), lanes) for j in range(4)]
        for k, piece in enumerate(turn_quarters(picked)):
            send_ref[4 * q + k, g] = piece


def pack_kernel(rim_ref, lanes_ref, send_ref):
    def one(q, carry):
        send_pieces(send_ref, lanes_ref, lambda l: rim_ref[l], rim_ref.shape[0], q)
        return carry

    lax.fori_loop(0, send_ref.shape[0] // 4, one, 0)


def prepare_kernel(home_ref, first_ref, second_ref, coef_ref):
    blocks, layers = coef_ref.shape[0], coef_ref.shape[2]
    side = first_ref.shape[0]
    y, x = home_ref[0], home_ref[1]

    def shifts(b):
        return lax.rem(y - b // side + side, side), lax.rem(x - lax.rem(b, side) + side, side)

    zero = jnp.zeros((1, LANES), jnp.float32)
    for start in range(0, blocks, 8):
        group = range(start, start + 8)
        at = {b: shifts(jnp.int32(b)) for b in group}
        ratio = {b: zero for b in group}
        lower = {b: zero for b in group}
        for l in range(layers):
            for b in group:
                hy, hx = at[b]
                upper = second_ref[hx, hy, layers + l : layers + l + 1, :]
                pivot = 1.0 + lower[b] + upper - lower[b] * ratio[b]
                inverse = 1.0 / pivot
                coef_ref[b, INV, l : l + 1, :] = inverse
                coef_ref[b, CARRY, l : l + 1, :] = lower[b] * inverse
                ratio[b] = upper * inverse
                lower[b] = upper

    def fill(b, carry):
        hy, hx = shifts(b)
        inverse = coef_ref[b, INV]
        coef_ref[b, RATIO] = second_ref[hx, hy, layers : 2 * layers] * inverse
        outflow = jnp.zeros((layers, LANES), jnp.float32)
        for f in range(3):
            if f < 2:
                flux = first_ref[hy, hx, f * layers : (f + 1) * layers]
            else:
                flux = second_ref[hx, hy, :layers]
            outflow = outflow + jnp.maximum(flux, 0.0)
            coef_ref[b, EDGE + f] = -jnp.minimum(flux, 0.0) * inverse
        coef_ref[b, OWN] = (1.0 - outflow) * inverse
        return carry

    lax.fori_loop(0, blocks, fill, 0)


def row(coef_ref, c, kind, l):
    return coef_ref[c, kind, pl.ds(l, 8, stride=0), :]


CHUNK = 20


def advect_block(plan_ref, load, coef_ref, near_ref, rate_ref, acc_ref, i, b, c, n, counts):
    layers = acc_ref.shape[1]
    width = plan_ref.shape[1]
    for l in range(layers):
        acc_ref[i, l] = jnp.zeros((8, LANES), jnp.float32)

    @pl.when(plan_ref[b, width - 1] > 0)
    def _():
        cell = b * LANES + lax.broadcasted_iota(jnp.int32, (8, LANES), 1)
        here = near_ref[n, 3] == cell
        for l in range(layers):
            acc_ref[i, l] = jnp.where(here, rate_ref[l], 0.0) * row(coef_ref, c, INV, l)

    def add_from(take):
        def one(k, carry):
            s = plan_ref[b, k]
            lanes = [near_ref[n, f] & (LANES - 1) for f in range(3)]
            inside = [(near_ref[n, f] >> 7) == s for f in range(3)]
            for start in range(0, layers, CHUNK):
                chunk = range(start, start + CHUNK)
                values = [take(k, s, l) for l in chunk]
                total = [acc_ref[i, l] for l in chunk]
                for f in range(3):
                    for j, l in enumerate(chunk):
                        edge = jnp.where(inside[f], pick_lanes(values[j], lanes[f]), 0.0)
                        total[j] = total[j] + row(coef_ref, c, EDGE + f, l) * edge
                for j, l in enumerate(chunk):
                    acc_ref[i, l] = total[j]
            return carry

        return one

    low = 0
    for take, high in zip(load, counts):
        lax.fori_loop(low, high, add_from(take), 0)
        low = high


def solve_blocks(own, coef_ref, acc_ref, store, where_coef):
    layers = acc_ref.shape[1]
    part = [None] * len(where_coef)
    for l in range(layers):
        for i, c in enumerate(where_coef):
            now = row(coef_ref, c, OWN, l) * own(i, l) + acc_ref[i, l]
            if l > 0:
                now = now + row(coef_ref, c, CARRY, l) * part[i]
            part[i] = now
            if l < layers - 1:
                acc_ref[i, l] = now
            else:
                store(i, l, now)
    for l in range(layers - 2, -1, -1):
        for i, c in enumerate(where_coef):
            part[i] = acc_ref[i, l] + row(coef_ref, c, RATIO, l) * part[i]
            store(i, l, part[i])


def lanes_of(b):
    return pl.ds(pl.multiple_of(b * LANES, LANES), LANES)


def rim_kernel(last, plan_ref, field_hbm, received_ref, coef_hbm, near_hbm, rate_hbm, *refs):
    if last:
        halo_hbm, new_hbm, *scratch = refs
    else:
        lanes_ref, send_hbm, halo_hbm, new_hbm, *scratch = refs
    source_ref, own_ref, coef_ref, near_ref, rate_ref, halo_ref, new_ref, acc_ref, *more = scratch
    in_sem, source_sem, out_sem = more[-3:]
    layers = acc_ref.shape[1]
    blocks = field_hbm.shape[2] // LANES
    rim = blocks - 1
    width = plan_ref.shape[1]
    local_count, all_count = plan_ref[rim, width - 3], plan_ref[rim, width - 2]

    def source_copy(k):
        return pltpu.make_async_copy(
            field_hbm.at[:, :, lanes_of(plan_ref[rim, k])], source_ref.at[k], source_sem.at[k]
        )

    loads = [
        pltpu.make_async_copy(coef_hbm.at[pl.ds(rim, 1)], coef_ref, in_sem.at[0]),
        pltpu.make_async_copy(near_hbm.at[pl.ds(rim, 1)], near_ref, in_sem.at[1]),
        pltpu.make_async_copy(rate_hbm, rate_ref, in_sem.at[2]),
        pltpu.make_async_copy(field_hbm.at[:, :, lanes_of(rim)], own_ref, in_sem.at[3]),
    ]
    for load in loads:
        load.start()

    def begin(k, carry):
        source_copy(k).start()
        return carry

    lax.fori_loop(0, local_count, begin, 0)
    quads = received_ref.shape[0] // 4

    def unpack(q, carry):
        for g in range(layers // 4):
            pieces = [received_ref[4 * q + k, g] for k in range(4)]
            for j, value in enumerate(turn_quarters(pieces)):
                halo_ref[q, 4 * g + j] = value
        return carry

    lax.fori_loop(0, quads, unpack, 0)
    halo_out = pltpu.make_async_copy(halo_ref, halo_hbm, out_sem.at[0])
    halo_out.start()
    for load in loads:
        load.wait()

    def end(k, carry):
        source_copy(k).wait()
        return carry

    lax.fori_loop(0, local_count, end, 0)
    advect_block(
        plan_ref,
        (lambda k, s, l: source_ref[k, l], lambda k, s, l: halo_ref[s - blocks, l]),
        coef_ref,
        near_ref,
        rate_ref,
        acc_ref,
        0,
        rim,
        0,
        0,
        (local_count, all_count),
    )

    def store(i, l, value):
        new_ref[l] = value

    solve_blocks(lambda i, l: own_ref[l], coef_ref, acc_ref, store, [0])
    new_out = pltpu.make_async_copy(new_ref, new_hbm, out_sem.at[1])
    new_out.start()
    if not last:
        send_ref = more[0]

        def message_copy(q):
            return pltpu.make_async_copy(
                send_ref.at[pl.ds(4 * q, 4)], send_hbm.at[pl.ds(4 * q, 4)], out_sem.at[2 + q]
            )

        def one(q, carry):
            send_pieces(send_ref, lanes_ref, lambda l: new_ref[l], layers, q)
            message_copy(q).start()
            return carry

        lax.fori_loop(0, quads, one, 0)
        for q in range(quads):
            message_copy(q).wait()
    halo_out.wait()
    new_out.wait()


GROUP = 5


def bulk_kernel(plan_ref, field_hbm, halo_hbm, rim_hbm, coef_hbm, near_hbm, rate_hbm, out_hbm, *refs):
    field_ref, halo_ref, coef_ref, near_ref, rate_ref, acc_ref, new_ref, in_sem, out_sem = refs
    blocks = field_hbm.shape[2] // LANES
    width = plan_ref.shape[1]
    groups = (blocks - 1) // GROUP
    span = GROUP * LANES

    def coef_copy(g):
        part = pl.ds(g * GROUP, GROUP)
        return pltpu.make_async_copy(coef_hbm.at[part], coef_ref.at[part], in_sem.at[4 + g])

    def out_copy(g):
        lanes = pl.ds(pl.multiple_of(g * span, span), span)
        return pltpu.make_async_copy(new_ref.at[:, :, lanes], out_hbm.at[:, :, lanes], out_sem.at[g])

    loads = [
        pltpu.make_async_copy(field_hbm, field_ref, in_sem.at[0]),
        pltpu.make_async_copy(near_hbm, near_ref, in_sem.at[1]),
        pltpu.make_async_copy(rate_hbm, rate_ref, in_sem.at[2]),
        pltpu.make_async_copy(halo_hbm, halo_ref, in_sem.at[3]),
    ]
    for load in loads:
        load.start()
    for g in range(groups):
        coef_copy(g).start()
    rim_out = pltpu.make_async_copy(
        rim_hbm, out_hbm.at[:, :, (blocks - 1) * LANES :], out_sem.at[groups]
    )
    rim_out.start()
    for load in loads:
        load.wait()

    def group(g, carry):
        coef_copy(g).wait()

        def advect(i, inner):
            b = g * GROUP + i
            advect_block(
                plan_ref,
                (
                    lambda k, s, l: field_ref[l, :, lanes_of(s)],
                    lambda k, s, l: halo_ref[s - blocks, l],
                ),
                coef_ref,
                near_ref,
                rate_ref,
                acc_ref,
                i,
                b,
                b,
                b,
                (plan_ref[b, width - 3], plan_ref[b, width - 2]),
            )
            return inner

        lax.fori_loop(0, GROUP, advect, 0)
        where = [g * GROUP + i for i in range(GROUP)]

        def store(i, l, value):
            new_ref[l, :, lanes_of(where[i])] = value

        solve_blocks(lambda i, l: field_ref[l, :, lanes_of(where[i])], coef_ref, acc_ref, store, where)
        out_copy(g).start()
        return carry

    lax.fori_loop(0, groups, group, 0)
    for g in range(groups):
        out_copy(g).wait()
    rim_out.wait()


def share_side(value, side):
    square = 4
    shifts = [value]
    for hop in range(1, square):
        pairs = []
        for y in range(square):
            for x in range(square):
                to = y * square + (x + hop) % square if side == 0 else (y + hop) % square * square + x
                pairs.append((y * square + x, to))
        shifts.append(lax.ppermute(value, "tracer", pairs))
    return jnp.stack(shifts)


def share(value):
    half = value.shape[0] // 2
    first = share_side(share_side(value[:half], 0), 1)
    second = share_side(share_side(value[half:], 1), 0)
    return first, second


def on_device(
    concentration, courant, diffusivity, release_rate, release_cell, neighbour, send_rows
):
    layers, tracers, cells = concentration.shape
    blocks = cells // LANES
    peers, slots = send_rows.shape[1], send_rows.shape[2]
    halo_cells = peers * slots
    rim = 64
    f32 = jnp.float32
    full = pl.BlockSpec(memory_space=VMEM)
    scalars = pl.BlockSpec(memory_space=SMEM)
    message = pltpu.HBM((peers, layers // 4, tracers, LANES), f32)

    def kept(value):
        return pltpu.with_memory_space_constraint(value, pltpu.HBM)

    def params(mib):
        return pltpu.CompilerParams(vmem_limit_bytes=mib << 20)

    def panel(h):
        empty = jnp.zeros((1, LANES), f32)
        rows = jnp.concatenate([courant[h].reshape(-1, LANES), diffusivity[h], empty], 0)
        return rows

    rows = LANES - rim + jnp.maximum(send_rows[0], 0)
    quads = peers * slots // LANES
    lanes = jnp.broadcast_to(rows.reshape(quads, 1, LANES), (quads, 8, LANES))

    send = pl.pallas_call(
        pack_kernel,
        out_shape=message,
        grid=(1,),
        in_specs=[
            pl.BlockSpec((layers, tracers, LANES), lambda i: (0, 0, blocks - 1)),
            pl.BlockSpec((quads, 8, LANES), lambda i: (0, 0, 0)),
        ],
        out_specs=pl.BlockSpec(message.shape, lambda i: (0, 0, 0, 0)),
        name="pack",
    )(concentration, lanes)
    received = lax.all_to_all(send, "region", 0, 0, tiled=True)
    tables = [share(panel(0)), None]

    sources = blocks + halo_cells // LANES
    of_block = neighbour.reshape(3, blocks, LANES)
    source_id = jnp.arange(sources, dtype=jnp.int32)
    needed = jnp.any((of_block[..., None] >> 7) == source_id, axis=(0, 2))
    rank = jnp.sum(
        needed[:, None, :] & (source_id[None, None, :] < source_id[None, :, None]), axis=2
    )
    listed = jnp.sum(
        jnp.where(
            needed[:, None, :] & (rank[:, None, :] == source_id[None, :, None]),
            source_id[None, None, :],
            0,
        ),
        axis=2,
    )
    home = release_cell - lax.axis_index("region") * cells
    released = jnp.any(
        (home[None, :] >> 7) == jnp.arange(blocks, dtype=jnp.int32)[:, None], axis=1
    )
    plan = jnp.concatenate(
        [
            listed,
            jnp.sum(needed[:, :blocks], axis=1)[:, None],
            jnp.sum(needed, axis=1)[:, None],
            released[:, None],
        ],
        axis=1,
    ).astype(jnp.int32)
    near = jnp.concatenate(
        [
            jnp.broadcast_to(jnp.moveaxis(of_block, 1, 0)[:, :, None, :], (blocks, 3, 8, LANES)),
            jnp.broadcast_to(home[None, None, :, None], (blocks, 1, 8, LANES)),
        ],
        axis=1,
    )
    near = kept(near)
    rate = kept(jnp.broadcast_to(release_rate[:, :, None], (layers, tracers, LANES)))

    coef_shape = (blocks, KINDS, layers, LANES)

    column = lax.axis_index("tracer")
    square = jnp.stack([column // 4, column % 4]).astype(jnp.int32)

    def prepare(table):
        return pl.pallas_call(
            prepare_kernel,
            out_shape=pltpu.HBM(coef_shape, f32),
            in_specs=[scalars, full, full],
            out_specs=full,
            compiler_params=params(16),
            name="prepare",
        )(square, *table)

    tile = (layers, tracers, LANES)
    new_block = pltpu.HBM(tile, f32)
    halo_shape = pltpu.HBM((quads, *tile), f32)
    hbm = pl.BlockSpec(memory_space=pltpu.HBM)
    dma = pltpu.SemaphoreType.DMA

    def rim_step(field, received, coef, last):
        outs = (halo_shape, new_block) if last else (message, halo_shape, new_block)
        vmem = pltpu.VMEM
        scratch = [
            vmem((blocks, *tile), f32),
            vmem(tile, f32),
            vmem((1, *coef_shape[1:]), f32),
            vmem((1, 4, 8, LANES), jnp.int32),
            vmem(tile, f32),
            vmem(halo_shape.shape, f32),
            vmem(tile, f32),
            vmem((1, *tile), f32),
        ]
        scratch += [] if last else [vmem(message.shape, f32)]
        scratch += [dma((4,)), dma((blocks,)), dma((2 + quads,))]
        result = pl.pallas_call(
            functools.partial(rim_kernel, last),
            out_shape=outs,
            in_specs=[scalars, hbm, full, hbm, hbm, hbm] + ([] if last else [full]),
            out_specs=(hbm,) * len(outs),
            scratch_shapes=scratch,
            compiler_params=params(16),
            name="rim",
        )(plan, kept(field), received, kept(coef), near, rate, *(() if last else (lanes,)))
        return result if not last else (None, *result)

    def bulk_step(field, halo, new, coef):
        vmem = pltpu.VMEM
        return pl.pallas_call(
            bulk_kernel,
            out_shape=pltpu.HBM(field.shape, f32),
            in_specs=[scalars] + [hbm] * 6,
            out_specs=hbm,
            scratch_shapes=[
                vmem(field.shape, f32),
                vmem(halo_shape.shape, f32),
                vmem(coef_shape, f32),
                vmem((blocks, 4, 8, LANES), jnp.int32),
                vmem(tile, f32),
                vmem((GROUP, *tile), f32),
                vmem(field.shape, f32),
                dma((4 + (blocks - 1) // GROUP,)),
                dma((1 + (blocks - 1) // GROUP,)),
            ],
            compiler_params=params(24),
            name="bulk",
        )(plan, kept(field), kept(halo), kept(new), kept(coef), near, rate)

    field = concentration
    per_hour = STEPS // HOURS
    coef = None
    for step in range(STEPS):
        h = step // per_hour
        if step % per_hour == 0:
            coef = prepare(tables[h])
        last = step == STEPS - 1
        send, halo, new = rim_step(field, received, coef, last)
        if step == 0:
            later = panel(1)
            later, _ = lax.optimization_barrier((later, new))
            tables[1] = share(later)
        if not last:
            received = lax.all_to_all(send, "region", 0, 0, tiled=True)
        field = bulk_step(field, halo, new, coef)
    return field


def solution(mesh):
    both = ("region", "tracer")
    return jax.shard_map(
        on_device,
        mesh=mesh,
        in_specs=(
            P(None, "tracer", "region"),
            P(None, None, None, both),
            P(None, None, both),
            P(None, "tracer"),
            P("tracer"),
            P(None, "region"),
            P("region", None, None),
        ),
        out_specs=P(None, "tracer", "region"),
        check_vma=False,
    )
```

```python
import functools
import jax
import jax.numpy as jnp
from jax import lax
from jax.experimental import pallas as pl
from jax.experimental.pallas import tpu as pltpu
from jax.sharding import PartitionSpec as P

HOURS = 2
STEPS = 6
LANES = 128
SMEM = pltpu.MemorySpace.SMEM
VMEM = pltpu.MemorySpace.VMEM

OWN, EDGE, CARRY, RATIO, INV = 0, 1, 4, 5, 6
KINDS = 7


def pick_lanes(values, lanes):
    return jnp.take_along_axis(values, lanes, axis=1, mode="promise_in_bounds")


def mix_quarters(parts, pieces, first):
    results = []
    for i in range(4):
        value = pieces[first(i) % 4]
        for p in range(1, 4):
            value = jnp.where(parts[p], pieces[(first(i) + p) % 4], value)
        results.append(value)
    return results


def quarter_masks():
    part = lax.broadcasted_iota(jnp.int32, (8, LANES), 1) // 32
    return [part == p for p in range(4)]


def send_pieces(send_ref, lanes_ref, load, layers, q):
    parts = quarter_masks()
    for g in range(layers // 4):
        picked = [pick_lanes(load(4 * g + j), lanes_ref[q, j]) for j in range(4)]
        for m, piece in enumerate(mix_quarters(parts, picked, lambda m: -m)):
            send_ref[4 * q + m, g] = piece


def unpack_pieces(halo_ref, received_ref, layers, q, own):
    parts = quarter_masks()
    for g in range(layers // 4):
        pieces = [received_ref[4 * q + k, g] for k in range(4)]
        turned = mix_quarters(parts, pieces, lambda d: -d)
        turned = [turned[0]] + [pltpu.roll(turned[d], LANES - 32 * d, 1) for d in range(1, 4)]
        backward = [turned[-k % 4] for k in range(4)]
        for p, value in enumerate(mix_quarters(parts, backward, lambda p: -p)):
            halo_ref[q, 4 * g + lax.rem(p - own + 4, 4)] = value


def pack_kernel(rim_ref, lanes_ref, send_ref):
    def one(q, carry):
        send_pieces(send_ref, lanes_ref, lambda l: rim_ref[l], rim_ref.shape[0], q)
        return carry

    lax.fori_loop(0, send_ref.shape[0] // 4, one, 0)


def prepare_kernel(home_ref, *refs):
    *panels, coef_ref = refs
    blocks, layers = coef_ref.shape[0], coef_ref.shape[2]
    side = panels[0].shape[0]
    y, x = home_ref[0], home_ref[1]

    def shifts(b):
        return lax.rem(y - b // side + side, side), lax.rem(x - lax.rem(b, side) + side, side)

    def rows(hy, hx, first, count):
        split = panels[0].shape[2]
        if first < split:
            return panels[0][hy, hx, first : first + count]
        return panels[1][hx, hy, first - split : first - split + count]

    zero = jnp.zeros((1, LANES), jnp.float32)
    for start in range(0, blocks, 8):
        group = range(start, start + 8)
        at = {b: shifts(jnp.int32(b)) for b in group}
        ratio = {b: zero for b in group}
        lower = {b: zero for b in group}
        for l in range(layers):
            for b in group:
                hy, hx = at[b]
                upper = rows(hy, hx, 3 * layers + l, 1)
                pivot = 1.0 + lower[b] + upper - lower[b] * ratio[b]
                inverse = 1.0 / pivot
                coef_ref[b, INV, l : l + 1, :] = inverse
                coef_ref[b, CARRY, l : l + 1, :] = lower[b] * inverse
                ratio[b] = upper * inverse
                lower[b] = upper

    def fill(b, carry):
        hy, hx = shifts(b)
        inverse = coef_ref[b, INV]
        coef_ref[b, RATIO] = rows(hy, hx, 3 * layers, layers) * inverse
        outflow = jnp.zeros((layers, LANES), jnp.float32)
        for f in range(3):
            flux = rows(hy, hx, f * layers, layers)
            outflow = outflow + jnp.maximum(flux, 0.0)
            coef_ref[b, EDGE + f] = -jnp.minimum(flux, 0.0) * inverse
        coef_ref[b, OWN] = (1.0 - outflow) * inverse
        return carry

    lax.fori_loop(0, blocks, fill, 0)


def row(coef_ref, c, kind, l):
    return coef_ref[c, kind, pl.ds(l, 8, stride=0), :]


CHUNK = 40


def advect_block(plan_ref, load, coef_ref, near_ref, rate_ref, acc_ref, i, b, c, n, counts):
    layers = acc_ref.shape[1]
    width = plan_ref.shape[1]
    for l in range(layers):
        acc_ref[i, l] = jnp.zeros((8, LANES), jnp.float32)

    @pl.when(plan_ref[b, width - 1] > 0)
    def _():
        cell = b * LANES + lax.broadcasted_iota(jnp.int32, (8, LANES), 1)
        here = near_ref[n, 3] == cell
        for l in range(layers):
            acc_ref[i, l] = jnp.where(here, rate_ref[l], 0.0) * row(coef_ref, c, INV, l)

    def add_from(take):
        def one(k, carry):
            lanes = [near_ref[n, f] & (LANES - 1) for f in range(3)]
            inside = [(near_ref[n, f] >> 7) == k for f in range(3)]
            from_first = near_ref[n, 4] != 0
            for start in range(0, layers, CHUNK):
                chunk = range(start, start + CHUNK)
                values = [take(k, from_first, l) for l in chunk]
                total = [acc_ref[i, l] for l in chunk]
                for f in range(3):
                    for j, l in enumerate(chunk):
                        edge = jnp.where(inside[f], pick_lanes(values[j], lanes[f]), 0.0)
                        total[j] = total[j] + row(coef_ref, c, EDGE + f, l) * edge
                for j, l in enumerate(chunk):
                    acc_ref[i, l] = total[j]
            return carry

        return one

    low = 0
    for take, high in zip(load, counts):
        lax.fori_loop(low, high, add_from(take), 0)
        low = high


def solve_blocks(own, coef_ref, acc_ref, store, where_coef):
    layers = acc_ref.shape[1]
    part = [None] * len(where_coef)
    for l in range(layers):
        for i, c in enumerate(where_coef):
            now = row(coef_ref, c, OWN, l) * own(i, l) + acc_ref[i, l]
            if l > 0:
                now = now + row(coef_ref, c, CARRY, l) * part[i]
            part[i] = now
            if l < layers - 1:
                acc_ref[i, l] = now
            else:
                store(i, l, now)
    for l in range(layers - 2, -1, -1):
        for i, c in enumerate(where_coef):
            part[i] = acc_ref[i, l] + row(coef_ref, c, RATIO, l) * part[i]
            store(i, l, part[i])


def lanes_of(b):
    return pl.ds(pl.multiple_of(b * LANES, LANES), LANES)


def rim_kernel(last, plan_ref, field_hbm, received_ref, coef_hbm, near_hbm, rate_hbm, *refs):
    if last:
        halo_hbm, new_hbm, *scratch = refs
    else:
        lanes_ref, send_hbm, halo_hbm, new_hbm, *scratch = refs
    source_ref, own_ref, coef_ref, near_ref, rate_ref, halo_ref, new_ref, acc_ref, *more = scratch
    in_sem, source_sem, out_sem = more[-3:]
    layers = acc_ref.shape[1]
    blocks = field_hbm.shape[2] // LANES
    rim = blocks - 1
    width = plan_ref.shape[1]
    local_count, all_count = plan_ref[rim, width - 3], plan_ref[rim, width - 2]

    pairs = (width - 4) // 2

    def source_copy(k, second):
        block = plan_ref[rim, pairs * second + k]
        to = 2 * k + second
        return pltpu.make_async_copy(
            field_hbm.at[:, :, lanes_of(block)], source_ref.at[to], source_sem.at[to]
        )

    def double(k):
        return plan_ref[rim, k] != plan_ref[rim, pairs + k]

    def take_local(k, from_first, l):
        other = 2 * k + double(k).astype(jnp.int32)
        return jnp.where(from_first, source_ref[2 * k, l], source_ref[other, l])

    loads = [
        pltpu.make_async_copy(coef_hbm.at[pl.ds(rim, 1)], coef_ref, in_sem.at[0]),
        pltpu.make_async_copy(near_hbm.at[pl.ds(rim, 1)], near_ref, in_sem.at[1]),
        pltpu.make_async_copy(rate_hbm, rate_ref, in_sem.at[2]),
        pltpu.make_async_copy(field_hbm.at[:, :, lanes_of(rim)], own_ref, in_sem.at[3]),
    ]
    for load in loads:
        load.start()

    def begin(k, carry):
        source_copy(k, 0).start()

        @pl.when(double(k))
        def _():
            source_copy(k, 1).start()

        return carry

    lax.fori_loop(0, local_count, begin, 0)
    quads = received_ref.shape[0] // 4

    def unpack(q, carry):
        unpack_pieces(halo_ref, received_ref, layers, q, plan_ref[rim, width - 4])
        return carry

    lax.fori_loop(0, quads, unpack, 0)
    halo_out = pltpu.make_async_copy(halo_ref, halo_hbm, out_sem.at[0])
    halo_out.start()
    for load in loads:
        load.wait()

    def end(k, carry):
        source_copy(k, 0).wait()

        @pl.when(double(k))
        def _():
            source_copy(k, 1).wait()

        return carry

    lax.fori_loop(0, local_count, end, 0)
    advect_block(
        plan_ref,
        (take_local, lambda k, from_first, l: halo_ref[plan_ref[rim, k] - blocks, l]),
        coef_ref,
        near_ref,
        rate_ref,
        acc_ref,
        0,
        rim,
        0,
        0,
        (local_count, all_count),
    )

    def store(i, l, value):
        new_ref[l] = value

    solve_blocks(lambda i, l: own_ref[l], coef_ref, acc_ref, store, [0])
    new_out = pltpu.make_async_copy(new_ref, new_hbm, out_sem.at[1])
    new_out.start()
    if not last:
        send_ref = more[0]

        def message_copy(q):
            return pltpu.make_async_copy(
                send_ref.at[pl.ds(4 * q, 4)], send_hbm.at[pl.ds(4 * q, 4)], out_sem.at[2 + q]
            )

        def one(q, carry):
            send_pieces(send_ref, lanes_ref, lambda l: new_ref[l], layers, q)
            message_copy(q).start()
            return carry

        lax.fori_loop(0, quads, one, 0)
        for q in range(quads):
            message_copy(q).wait()
    halo_out.wait()
    new_out.wait()


GROUP = 5


def bulk_kernel(
    plan_ref, field_hbm, halo_hbm, rim_hbm, coef_hbm, near_hbm, rate_hbm, early_hbm, out_hbm, *refs
):
    del early_hbm
    field_ref, halo_ref, coef_ref, near_ref, rate_ref, acc_ref, new_ref, in_sem, out_sem = refs
    blocks = field_hbm.shape[2] // LANES
    width = plan_ref.shape[1]
    pairs = (width - 4) // 2
    groups = (blocks - 1) // GROUP
    span = GROUP * LANES

    def coef_copy(g):
        part = pl.ds(g * GROUP, GROUP)
        return pltpu.make_async_copy(coef_hbm.at[part], coef_ref.at[part], in_sem.at[4 + g])

    def out_copy(g):
        lanes = pl.ds(pl.multiple_of(g * span, span), span)
        return pltpu.make_async_copy(new_ref.at[:, :, lanes], out_hbm.at[:, :, lanes], out_sem.at[g])

    loads = [
        pltpu.make_async_copy(field_hbm, field_ref, in_sem.at[0]),
        pltpu.make_async_copy(near_hbm, near_ref, in_sem.at[1]),
        pltpu.make_async_copy(rate_hbm, rate_ref, in_sem.at[2]),
        pltpu.make_async_copy(halo_hbm, halo_ref, in_sem.at[3]),
    ]
    for load in loads:
        load.start()
    for g in range(groups):
        coef_copy(g).start()
    rim_out = pltpu.make_async_copy(
        rim_hbm, out_hbm.at[:, :, (blocks - 1) * LANES :], out_sem.at[groups]
    )
    rim_out.start()
    for load in loads:
        load.wait()

    def group(g, carry):
        coef_copy(g).wait()

        def advect(i, inner):
            b = g * GROUP + i
            advect_block(
                plan_ref,
                (
                    lambda k, from_first, l: jnp.where(
                        from_first,
                        field_ref[l, :, lanes_of(plan_ref[b, k])],
                        field_ref[l, :, lanes_of(plan_ref[b, pairs + k])],
                    ),
                    lambda k, from_first, l: halo_ref[plan_ref[b, k] - blocks, l],
                ),
                coef_ref,
                near_ref,
                rate_ref,
                acc_ref,
                i,
                b,
                b,
                b,
                (plan_ref[b, width - 3], plan_ref[b, width - 2]),
            )
            return inner

        lax.fori_loop(0, GROUP, advect, 0)
        where = [g * GROUP + i for i in range(GROUP)]

        def store(i, l, value):
            new_ref[l, :, lanes_of(where[i])] = value

        solve_blocks(lambda i, l: field_ref[l, :, lanes_of(where[i])], coef_ref, acc_ref, store, where)
        out_copy(g).start()
        return carry

    lax.fori_loop(0, groups, group, 0)
    for g in range(groups):
        out_copy(g).wait()
    rim_out.wait()


def share_side(value, side):
    square = 4
    shifts = [value]
    for hop in range(1, square):
        pairs = []
        for y in range(square):
            for x in range(square):
                to = y * square + (x + hop) % square if side == 0 else (y + hop) % square * square + x
                pairs.append((y * square + x, to))
        shifts.append(lax.ppermute(value, "tracer", pairs))
    return jnp.stack(shifts)


def share(value):
    half = value.shape[0] // 2
    first = share_side(share_side(value[:half], 0), 1)
    second = share_side(share_side(value[half:], 1), 0)
    return first, second


def transport(
    concentration, courant, diffusivity, release_rate, release_cell, neighbour, send_rows
):
    layers, tracers, cells = concentration.shape
    blocks = cells // LANES
    peers, slots = send_rows.shape[1], send_rows.shape[2]
    halo_cells = peers * slots
    rim = 64
    f32 = jnp.float32
    full = pl.BlockSpec(memory_space=VMEM)
    scalars = pl.BlockSpec(memory_space=SMEM)
    message = pltpu.HBM((peers, layers // 4, tracers, LANES), f32)

    def kept(value):
        return pltpu.with_memory_space_constraint(value, pltpu.HBM)

    def params(mib):
        return pltpu.CompilerParams(vmem_limit_bytes=mib << 20)

    def panel(h):
        empty = jnp.zeros((1, LANES), f32)
        rows = jnp.concatenate([courant[h].reshape(-1, LANES), diffusivity[h], empty], 0)
        return rows

    rows = LANES - rim + jnp.maximum(send_rows[0], 0)
    quads = peers * slots // LANES
    of_quad = rows.reshape(quads, 4, slots)
    turned = jnp.stack([jnp.roll(of_quad, j, axis=1) for j in range(4)], axis=1)
    lanes = jnp.broadcast_to(turned.reshape(quads, 4, 1, LANES), (quads, 4, 8, LANES))

    send = pl.pallas_call(
        pack_kernel,
        out_shape=message,
        grid=(1,),
        in_specs=[
            pl.BlockSpec((layers, tracers, LANES), lambda i: (0, 0, blocks - 1)),
            pl.BlockSpec((quads, 4, 8, LANES), lambda i: (0, 0, 0, 0)),
        ],
        out_specs=pl.BlockSpec(message.shape, lambda i: (0, 0, 0, 0)),
        name="pack",
    )(concentration, lanes)
    received = lax.all_to_all(send, "region", 0, 0, tiled=True)

    sources = blocks + halo_cells // LANES
    of_block = neighbour.reshape(3, blocks, LANES)
    source_id = jnp.arange(sources, dtype=jnp.int32)
    needed = jnp.any((of_block[..., None] >> 7) == source_id, axis=(0, 2))
    block_id = jnp.arange(blocks, dtype=jnp.int32)
    before, after = (block_id - 1) % blocks, (block_id + 1) % blocks
    entries = jnp.moveaxis(of_block, 1, 0).reshape(blocks, 3 * LANES, 1)
    lane_id = jnp.arange(LANES, dtype=jnp.int32)

    def wanted(source):
        return jnp.any(entries == source[:, None, None] * LANES + lane_id, axis=1)

    want_before, want_after = wanted(before), wanted(after)
    merged = (
        jnp.any(want_before, axis=1)
        & jnp.any(want_after, axis=1)
        & ~jnp.any(want_before & want_after, axis=1)
    )
    second = merged[:, None] & (source_id == after[:, None])
    needed = needed & ~second
    rank = jnp.sum(
        needed[:, None, :] & (source_id[None, None, :] < source_id[None, :, None]), axis=2
    )
    place = jnp.where(
        second, jnp.sum(jnp.where(source_id == before[:, None], rank, 0), axis=1)[:, None], rank
    )
    listed = jnp.sum(
        jnp.where(
            needed[:, None, :] & (rank[:, None, :] == source_id[None, :, None]),
            source_id[None, None, :],
            0,
        ),
        axis=2,
    )
    also = jnp.where(merged[:, None] & (listed == before[:, None]), after[:, None], listed)
    place_of = jnp.sum(
        jnp.where((of_block[..., None] >> 7) == source_id, place[None, :, None, :], 0), axis=3
    )
    near_id = jnp.where(of_block < 0, -1, place_of * LANES + (of_block & (LANES - 1)))
    home = release_cell - lax.axis_index("region") * cells
    released = jnp.any(
        (home[None, :] >> 7) == jnp.arange(blocks, dtype=jnp.int32)[:, None], axis=1
    )
    plan = jnp.concatenate(
        [
            listed,
            also,
            jnp.broadcast_to(lax.axis_index("region") % 4, (blocks, 1)),
            jnp.sum(needed[:, :blocks], axis=1)[:, None],
            jnp.sum(needed, axis=1)[:, None],
            released[:, None],
        ],
        axis=1,
    ).astype(jnp.int32)
    near = jnp.concatenate(
        [
            jnp.broadcast_to(jnp.moveaxis(near_id, 1, 0)[:, :, None, :], (blocks, 3, 8, LANES)),
            jnp.broadcast_to(home[None, None, :, None], (blocks, 1, 8, LANES)),
            jnp.broadcast_to(want_before[:, None, None, :], (blocks, 1, 8, LANES)).astype(jnp.int32),
        ],
        axis=1,
    )
    near = kept(near)
    rate = kept(jnp.broadcast_to(release_rate[:, :, None], (layers, tracers, LANES)))

    coef_shape = (blocks, KINDS, layers, LANES)

    column = lax.axis_index("tracer")
    square = jnp.stack([column // 4, column % 4]).astype(jnp.int32)

    def prepare(table):
        return pl.pallas_call(
            prepare_kernel,
            out_shape=pltpu.HBM(coef_shape, f32),
            in_specs=[scalars] + [full] * len(table),
            out_specs=full,
            compiler_params=params(16),
            name="prepare",
        )(square, *table)

    tile = (layers, tracers, LANES)
    new_block = pltpu.HBM(tile, f32)
    halo_shape = pltpu.HBM((quads, *tile), f32)
    hbm = pl.BlockSpec(memory_space=pltpu.HBM)
    dma = pltpu.SemaphoreType.DMA

    def rim_step(field, received, coef, last):
        outs = (halo_shape, new_block) if last else (message, halo_shape, new_block)
        vmem = pltpu.VMEM
        scratch = [
            vmem((2 * blocks, *tile), f32),
            vmem(tile, f32),
            vmem((1, *coef_shape[1:]), f32),
            vmem((1, 5, 8, LANES), jnp.int32),
            vmem(tile, f32),
            vmem(halo_shape.shape, f32),
            vmem(tile, f32),
            vmem((1, *tile), f32),
        ]
        scratch += [] if last else [vmem(message.shape, f32)]
        scratch += [dma((4,)), dma((2 * blocks,)), dma((2 + quads,))]
        result = pl.pallas_call(
            functools.partial(rim_kernel, last),
            out_shape=outs,
            in_specs=[scalars, hbm, full, hbm, hbm, hbm] + ([] if last else [full]),
            out_specs=(hbm,) * len(outs),
            scratch_shapes=scratch,
            compiler_params=params(20),
            name="rim",
        )(plan, kept(field), received, kept(coef), near, rate, *(() if last else (lanes,)))
        return result if not last else (None, *result)

    def bulk_step(field, halo, new, coef, early):
        vmem = pltpu.VMEM
        return pl.pallas_call(
            bulk_kernel,
            out_shape=pltpu.HBM(field.shape, f32),
            in_specs=[scalars] + [hbm] * 7,
            out_specs=hbm,
            scratch_shapes=[
                vmem(field.shape, f32),
                vmem(halo_shape.shape, f32),
                vmem(coef_shape, f32),
                vmem((blocks, 5, 8, LANES), jnp.int32),
                vmem(tile, f32),
                vmem((GROUP, *tile), f32),
                vmem(field.shape, f32),
                dma((4 + (blocks - 1) // GROUP,)),
                dma((1 + (blocks - 1) // GROUP,)),
            ],
            compiler_params=params(24),
            name="bulk",
        )(plan, kept(field), kept(halo), kept(new), kept(coef), near, rate, kept(early))

    field = concentration
    per_hour = STEPS // HOURS
    coef = prepare(share(panel(0)))
    for step in range(STEPS):
        last = step == STEPS - 1
        early = rate
        send, halo, new = rim_step(field, received, coef, last)
        if not last:
            received = lax.all_to_all(send, "region", 0, 0, tiled=True)
        if step == 0:
            later, _ = lax.optimization_barrier((panel(1), new))
            row_panels = share_side(later, 0)
        if step == 1:
            panels = share_side(row_panels, 1)
        if step == per_hour - 1:
            early = later_coef = prepare((panels,))
        field = bulk_step(field, halo, new, coef, early)
        if step == per_hour - 1:
            coef = later_coef
    return field


def solution(mesh):
    both = ("region", "tracer")
    return jax.shard_map(
        transport,
        mesh=mesh,
        in_specs=(
            P(None, "tracer", "region"),
            P(None, None, None, both),
            P(None, None, both),
            P(None, "tracer"),
            P("tracer"),
            P(None, "region"),
            P("region", None, None),
        ),
        out_specs=P(None, "tracer", "region"),
        check_vma=False,
    )
```

```python
import functools
import jax
import jax.numpy as jnp
from jax import lax
from jax.experimental import pallas as pl
from jax.experimental.pallas import tpu as pltpu
from jax.sharding import PartitionSpec as P

HOURS = 2
STEPS = 6
LANES = 128
SMEM = pltpu.MemorySpace.SMEM
VMEM = pltpu.MemorySpace.VMEM

OWN, EDGE, CARRY, RATIO, INV = 0, 1, 4, 5, 6
KINDS = 7


def pick_lanes(values, lanes):
    return jnp.take_along_axis(values, lanes, axis=1, mode="promise_in_bounds")


def mix_quarters(parts, pieces, first):
    results = []
    for i in range(4):
        value = pieces[first(i) % 4]
        for p in range(1, 4):
            value = jnp.where(parts[p], pieces[(first(i) + p) % 4], value)
        results.append(value)
    return results


def quarter_masks():
    part = lax.broadcasted_iota(jnp.int32, (8, LANES), 1) // 32
    return [part == p for p in range(4)]


def send_pieces(send_ref, lanes_ref, load, layers, q):
    parts = quarter_masks()
    for g in range(layers // 4):
        picked = [pick_lanes(load(4 * g + j), lanes_ref[q, j]) for j in range(4)]
        for m, piece in enumerate(mix_quarters(parts, picked, lambda m: -m)):
            send_ref[4 * q + m, g] = piece


def unpack_pieces(halo_ref, received_ref, layers, q, own):
    parts = quarter_masks()
    for g in range(layers // 4):
        pieces = [received_ref[4 * q + k, g] for k in range(4)]
        turned = mix_quarters(parts, pieces, lambda d: -d)
        turned = [turned[0]] + [pltpu.roll(turned[d], LANES - 32 * d, 1) for d in range(1, 4)]
        backward = [turned[-k % 4] for k in range(4)]
        for p, value in enumerate(mix_quarters(parts, backward, lambda p: -p)):
            halo_ref[q, 4 * g + lax.rem(p - own + 4, 4)] = value


def pack_kernel(rim_ref, lanes_ref, send_ref):
    def one(q, carry):
        send_pieces(send_ref, lanes_ref, lambda l: rim_ref[l], rim_ref.shape[0], q)
        return carry

    lax.fori_loop(0, send_ref.shape[0] // 4, one, 0)


def prepare_kernel(home_ref, *refs):
    *panels, coef_ref = refs
    blocks, layers = coef_ref.shape[0], coef_ref.shape[2]
    side = panels[0].shape[0]
    y, x = home_ref[0], home_ref[1]

    def shifts(b):
        return lax.rem(y - b // side + side, side), lax.rem(x - lax.rem(b, side) + side, side)

    def rows(hy, hx, first, count):
        split = panels[0].shape[2]
        if first < split:
            return panels[0][hy, hx, first : first + count]
        return panels[1][hx, hy, first - split : first - split + count]

    zero = jnp.zeros((1, LANES), jnp.float32)
    for start in range(0, blocks, 8):
        group = range(start, start + 8)
        at = {b: shifts(jnp.int32(b)) for b in group}
        ratio = {b: zero for b in group}
        lower = {b: zero for b in group}
        for l in range(layers):
            for b in group:
                hy, hx = at[b]
                upper = rows(hy, hx, 3 * layers + l, 1)
                pivot = 1.0 + lower[b] + upper - lower[b] * ratio[b]
                inverse = 1.0 / pivot
                coef_ref[b, INV, l : l + 1, :] = inverse
                coef_ref[b, CARRY, l : l + 1, :] = lower[b] * inverse
                ratio[b] = upper * inverse
                lower[b] = upper

    def fill(b, carry):
        hy, hx = shifts(b)
        inverse = coef_ref[b, INV]
        coef_ref[b, RATIO] = rows(hy, hx, 3 * layers, layers) * inverse
        outflow = jnp.zeros((layers, LANES), jnp.float32)
        for f in range(3):
            flux = rows(hy, hx, f * layers, layers)
            outflow = outflow + jnp.maximum(flux, 0.0)
            coef_ref[b, EDGE + f] = -jnp.minimum(flux, 0.0) * inverse
        coef_ref[b, OWN] = (1.0 - outflow) * inverse
        return carry

    lax.fori_loop(0, blocks, fill, 0)


def row(coef_ref, c, kind, l):
    return coef_ref[c, kind, pl.ds(l, 8, stride=0), :]


def start_block(plan_ref, coef_ref, near_ref, rate_ref, acc_ref, i, b, c, n):
    layers = acc_ref.shape[1]
    width = plan_ref.shape[1]
    for l in range(layers):
        acc_ref[i, l] = jnp.zeros((8, LANES), jnp.float32)

    @pl.when(plan_ref[b, width - 1] > 0)
    def _():
        cell = b * LANES + lax.broadcasted_iota(jnp.int32, (8, LANES), 1)
        here = near_ref[n, 3] == cell
        for l in range(layers):
            acc_ref[i, l] = jnp.where(here, rate_ref[l], 0.0) * row(coef_ref, c, INV, l)


def add_edges(take, coef_ref, near_ref, acc_ref, i, c, n, low, high):
    layers = acc_ref.shape[1]

    def one(k, carry):
        lanes = [near_ref[n, f] & (LANES - 1) for f in range(3)]
        inside = [(near_ref[n, f] >> 7) == k for f in range(3)]
        from_first = near_ref[n, 4] != 0
        values = [take(k, from_first, l) for l in range(layers)]
        total = [acc_ref[i, l] for l in range(layers)]
        for f in range(3):
            for l in range(layers):
                edge = jnp.where(inside[f], pick_lanes(values[l], lanes[f]), 0.0)
                total[l] = total[l] + row(coef_ref, c, EDGE + f, l) * edge
        for l in range(layers):
            acc_ref[i, l] = total[l]
        return carry

    lax.fori_loop(low, high, one, 0)


def advect_block(plan_ref, load, coef_ref, near_ref, rate_ref, acc_ref, i, b, c, n, counts):
    start_block(plan_ref, coef_ref, near_ref, rate_ref, acc_ref, i, b, c, n)
    low = 0
    for take, high in zip(load, counts):
        add_edges(take, coef_ref, near_ref, acc_ref, i, c, n, low, high)
        low = high


def solve_blocks(own, coef_ref, acc_ref, store, where_coef):
    layers = acc_ref.shape[1]
    part = [None] * len(where_coef)
    for l in range(layers):
        for i, c in enumerate(where_coef):
            now = own(i, l, c) + acc_ref[i, l]
            if l > 0:
                now = now + row(coef_ref, c, CARRY, l) * part[i]
            part[i] = now
            if l < layers - 1:
                acc_ref[i, l] = now
            else:
                store(i, l, now)
    for l in range(layers - 2, -1, -1):
        for i, c in enumerate(where_coef):
            part[i] = acc_ref[i, l] + row(coef_ref, c, RATIO, l) * part[i]
            store(i, l, part[i])


def solve_parts(coef_ref, acc_ref, store, where):
    layers = acc_ref.shape[1]
    part = [None] * len(where)
    for l in range(layers):
        for i, b in enumerate(where):
            now = acc_ref[b, l]
            if l > 0:
                now = now + row(coef_ref, b, CARRY, l) * part[i]
            part[i] = now
            if l < layers - 1:
                acc_ref[b, l] = now
            else:
                store(i, l, now)
    for l in range(layers - 2, -1, -1):
        for i, b in enumerate(where):
            part[i] = acc_ref[b, l] + row(coef_ref, b, RATIO, l) * part[i]
            store(i, l, part[i])


def lanes_of(b):
    return pl.ds(pl.multiple_of(b * LANES, LANES), LANES)


def rim_kernel(last, plan_ref, field_hbm, received_ref, coef_hbm, near_hbm, rate_hbm, *refs):
    if last:
        halo_hbm, new_hbm, *scratch = refs
    else:
        lanes_ref, send_hbm, halo_hbm, new_hbm, *scratch = refs
    source_ref, own_ref, coef_ref, near_ref, rate_ref, halo_ref, new_ref, acc_ref, *more = scratch
    in_sem, source_sem, out_sem = more[-3:]
    layers = acc_ref.shape[1]
    blocks = field_hbm.shape[2] // LANES
    rim = blocks - 1
    width = plan_ref.shape[1]
    local_count, all_count = plan_ref[rim, width - 3], plan_ref[rim, width - 2]

    pairs = (width - 4) // 2

    def source_copy(k, second):
        block = plan_ref[rim, pairs * second + k]
        to = 2 * k + second
        return pltpu.make_async_copy(
            field_hbm.at[:, :, lanes_of(block)], source_ref.at[to], source_sem.at[to]
        )

    def double(k):
        return plan_ref[rim, k] != plan_ref[rim, pairs + k]

    def take_local(k, from_first, l):
        other = 2 * k + double(k).astype(jnp.int32)
        return jnp.where(from_first, source_ref[2 * k, l], source_ref[other, l])

    loads = [
        pltpu.make_async_copy(coef_hbm.at[pl.ds(rim, 1)], coef_ref, in_sem.at[0]),
        pltpu.make_async_copy(near_hbm.at[pl.ds(rim, 1)], near_ref, in_sem.at[1]),
        pltpu.make_async_copy(rate_hbm, rate_ref, in_sem.at[2]),
        pltpu.make_async_copy(field_hbm.at[:, :, lanes_of(rim)], own_ref, in_sem.at[3]),
    ]
    for load in loads:
        load.start()

    def begin(k, carry):
        source_copy(k, 0).start()

        @pl.when(double(k))
        def _():
            source_copy(k, 1).start()

        return carry

    lax.fori_loop(0, local_count, begin, 0)
    quads = received_ref.shape[0] // 4

    def unpack(q, carry):
        unpack_pieces(halo_ref, received_ref, layers, q, plan_ref[rim, width - 4])
        return carry

    lax.fori_loop(0, quads, unpack, 0)
    halo_out = pltpu.make_async_copy(halo_ref, halo_hbm, out_sem.at[0])
    halo_out.start()
    for load in loads:
        load.wait()

    def end(k, carry):
        source_copy(k, 0).wait()

        @pl.when(double(k))
        def _():
            source_copy(k, 1).wait()

        return carry

    lax.fori_loop(0, local_count, end, 0)
    advect_block(
        plan_ref,
        (take_local, lambda k, from_first, l: halo_ref[plan_ref[rim, k] - blocks, l]),
        coef_ref,
        near_ref,
        rate_ref,
        acc_ref,
        0,
        rim,
        0,
        0,
        (local_count, all_count),
    )

    def store(i, l, value):
        new_ref[l] = value

    def own(i, l, c):
        return row(coef_ref, c, OWN, l) * own_ref[l]

    solve_blocks(own, coef_ref, acc_ref, store, [0])
    new_out = pltpu.make_async_copy(new_ref, new_hbm, out_sem.at[1])
    new_out.start()
    if not last:
        send_ref = more[0]

        def message_copy(q):
            return pltpu.make_async_copy(
                send_ref.at[pl.ds(4 * q, 4)], send_hbm.at[pl.ds(4 * q, 4)], out_sem.at[2 + q]
            )

        def one(q, carry):
            send_pieces(send_ref, lanes_ref, lambda l: new_ref[l], layers, q)
            message_copy(q).start()
            return carry

        lax.fori_loop(0, quads, one, 0)
        for q in range(quads):
            message_copy(q).wait()
    halo_out.wait()
    new_out.wait()


GROUP = 5


def bulk_kernel(
    plan_ref, field_hbm, halo_hbm, rim_hbm, coef_hbm, near_hbm, rate_hbm, early_hbm, out_hbm, *refs
):
    del early_hbm
    field_ref, halo_ref, coef_ref, near_ref, rate_ref, acc_ref, new_ref, in_sem, out_sem = refs
    blocks = field_hbm.shape[2] // LANES
    width = plan_ref.shape[1]
    pairs = (width - 4) // 2
    groups = (blocks - 1) // GROUP
    span = GROUP * LANES

    def coef_copy(g):
        part = pl.ds(g * GROUP, GROUP)
        return pltpu.make_async_copy(coef_hbm.at[part], coef_ref.at[part], in_sem.at[4 + g])

    def out_copy(g):
        lanes = pl.ds(pl.multiple_of(g * span, span), span)
        return pltpu.make_async_copy(new_ref.at[:, :, lanes], out_hbm.at[:, :, lanes], out_sem.at[g])

    loads = [
        pltpu.make_async_copy(field_hbm, field_ref, in_sem.at[0]),
        pltpu.make_async_copy(near_hbm, near_ref, in_sem.at[1]),
        pltpu.make_async_copy(rate_hbm, rate_ref, in_sem.at[2]),
        pltpu.make_async_copy(halo_hbm, halo_ref, in_sem.at[3]),
    ]
    for load in loads:
        load.start()
    for g in range(groups):
        coef_copy(g).start()
    rim_out = pltpu.make_async_copy(
        rim_hbm, out_hbm.at[:, :, (blocks - 1) * LANES :], out_sem.at[groups]
    )
    rim_out.start()
    for load in loads:
        load.wait()

    def group(g, carry):
        coef_copy(g).wait()

        def advect(i, inner):
            b = g * GROUP + i
            advect_block(
                plan_ref,
                (
                    lambda k, from_first, l: jnp.where(
                        from_first,
                        field_ref[l, :, lanes_of(plan_ref[b, k])],
                        field_ref[l, :, lanes_of(plan_ref[b, pairs + k])],
                    ),
                    lambda k, from_first, l: halo_ref[plan_ref[b, k] - blocks, l],
                ),
                coef_ref,
                near_ref,
                rate_ref,
                acc_ref,
                i,
                b,
                b,
                b,
                (plan_ref[b, width - 3], plan_ref[b, width - 2]),
            )
            return inner

        lax.fori_loop(0, GROUP, advect, 0)
        where = [g * GROUP + i for i in range(GROUP)]

        def store(i, l, value):
            new_ref[l, :, lanes_of(where[i])] = value

        def own(i, l, c):
            return row(coef_ref, c, OWN, l) * field_ref[l, :, lanes_of(where[i])]

        solve_blocks(own, coef_ref, acc_ref, store, where)
        out_copy(g).start()
        return carry

    lax.fori_loop(0, groups, group, 0)
    for g in range(groups):
        out_copy(g).wait()
    rim_out.wait()


def local_kernel(plan_ref, field_hbm, coef_hbm, near_hbm, rate_hbm, part_hbm, *refs):
    field_ref, coef_ref, near_ref, rate_ref, acc_ref, in_sem, out_sem = refs
    blocks, layers = acc_ref.shape[0], acc_ref.shape[1]
    width = plan_ref.shape[1]
    pairs = (width - 4) // 2
    loads = [
        pltpu.make_async_copy(field_hbm, field_ref, in_sem.at[0]),
        pltpu.make_async_copy(near_hbm, near_ref, in_sem.at[1]),
        pltpu.make_async_copy(rate_hbm, rate_ref, in_sem.at[2]),
        pltpu.make_async_copy(coef_hbm, coef_ref, in_sem.at[3]),
    ]
    for load in loads:
        load.start()
    for load in loads:
        load.wait()

    def out_copy(b):
        return pltpu.make_async_copy(acc_ref.at[b], part_hbm.at[b], out_sem.at[b])

    def block(b, carry):
        start_block(plan_ref, coef_ref, near_ref, rate_ref, acc_ref, b, b, b, b)

        def take(k, from_first, l):
            return jnp.where(
                from_first,
                field_ref[l, :, lanes_of(plan_ref[b, k])],
                field_ref[l, :, lanes_of(plan_ref[b, pairs + k])],
            )

        add_edges(take, coef_ref, near_ref, acc_ref, b, b, b, 0, plan_ref[b, width - 3])
        for l in range(layers):
            own = row(coef_ref, b, OWN, l) * field_ref[l, :, lanes_of(b)]
            acc_ref[b, l] = acc_ref[b, l] + own
        out_copy(b).start()
        return carry

    lax.fori_loop(0, blocks, block, 0)

    def finish(b, carry):
        out_copy(b).wait()
        return carry

    lax.fori_loop(0, blocks, finish, 0)


def finish_kernel(plan_ref, part_hbm, received_ref, coef_hbm, near_hbm, out_hbm, *refs):
    acc_ref, coef_ref, near_ref, halo_ref, new_ref, in_sem, out_sem = refs
    blocks, layers = acc_ref.shape[0], acc_ref.shape[1]
    width = plan_ref.shape[1]
    group = 4
    span = group * LANES
    near_copy = pltpu.make_async_copy(near_hbm, near_ref, in_sem.at[0])
    near_copy.start()

    def copies(g):
        part = pl.ds(g * group, group)
        return (
            pltpu.make_async_copy(part_hbm.at[part], acc_ref.at[part], in_sem.at[1 + 2 * g]),
            pltpu.make_async_copy(coef_hbm.at[part], coef_ref.at[part], in_sem.at[2 + 2 * g]),
        )

    def out_copy(g):
        lanes = pl.ds(pl.multiple_of(g * span, span), span)
        return pltpu.make_async_copy(new_ref.at[:, :, lanes], out_hbm.at[:, :, lanes], out_sem.at[g])

    groups = blocks // group
    for g in range(groups):
        for copy in copies(g):
            copy.start()

    def unpack(q, carry):
        unpack_pieces(halo_ref, received_ref, layers, q, plan_ref[0, width - 4])
        return carry

    lax.fori_loop(0, halo_ref.shape[0], unpack, 0)
    near_copy.wait()

    def one(g, carry):
        for copy in copies(g):
            copy.wait()

        def edges(i, inner):
            b = g * group + i
            add_edges(
                lambda k, from_first, l: halo_ref[plan_ref[b, k] - blocks, l],
                coef_ref,
                near_ref,
                acc_ref,
                b,
                b,
                b,
                plan_ref[b, width - 3],
                plan_ref[b, width - 2],
            )
            return inner

        lax.fori_loop(0, group, edges, 0)
        where = [g * group + i for i in range(group)]

        def store(i, l, value):
            new_ref[l, :, lanes_of(where[i])] = value

        solve_parts(coef_ref, acc_ref, store, where)
        out_copy(g).start()
        return carry

    lax.fori_loop(0, groups, one, 0)
    for g in range(groups):
        out_copy(g).wait()


def share_side(value, side):
    square = 4
    shifts = [value]
    for hop in range(1, square):
        pairs = []
        for y in range(square):
            for x in range(square):
                to = y * square + (x + hop) % square if side == 0 else (y + hop) % square * square + x
                pairs.append((y * square + x, to))
        shifts.append(lax.ppermute(value, "tracer", pairs))
    return jnp.stack(shifts)


def share(value):
    half = value.shape[0] // 2
    first, second = share_side(value[:half], 0), share_side(value[half:], 1)
    first, second = share_side(first, 1), share_side(second, 0)
    return first, second


def transport(
    concentration, courant, diffusivity, release_rate, release_cell, neighbour, send_rows
):
    layers, tracers, cells = concentration.shape
    blocks = cells // LANES
    peers, slots = send_rows.shape[1], send_rows.shape[2]
    halo_cells = peers * slots
    rim = 64
    f32 = jnp.float32
    full = pl.BlockSpec(memory_space=VMEM)
    scalars = pl.BlockSpec(memory_space=SMEM)
    message = pltpu.HBM((peers, layers // 4, tracers, LANES), f32)

    def kept(value):
        return pltpu.with_memory_space_constraint(value, pltpu.HBM)

    def params(mib):
        return pltpu.CompilerParams(vmem_limit_bytes=mib << 20)

    def panel(h):
        empty = jnp.zeros((1, LANES), f32)
        rows = jnp.concatenate([courant[h].reshape(-1, LANES), diffusivity[h], empty], 0)
        return rows

    rows = LANES - rim + jnp.maximum(send_rows[0], 0)
    quads = peers * slots // LANES
    of_quad = rows.reshape(quads, 4, slots)
    turned = jnp.stack([jnp.roll(of_quad, j, axis=1) for j in range(4)], axis=1)
    lanes = jnp.broadcast_to(turned.reshape(quads, 4, 1, LANES), (quads, 4, 8, LANES))

    send = pl.pallas_call(
        pack_kernel,
        out_shape=message,
        grid=(1,),
        in_specs=[
            pl.BlockSpec((layers, tracers, LANES), lambda i: (0, 0, blocks - 1)),
            pl.BlockSpec((quads, 4, 8, LANES), lambda i: (0, 0, 0, 0)),
        ],
        out_specs=pl.BlockSpec(message.shape, lambda i: (0, 0, 0, 0)),
        name="pack",
    )(concentration, lanes)
    received = lax.all_to_all(send, "region", 0, 0, tiled=True)

    sources = blocks + halo_cells // LANES
    of_block = neighbour.reshape(3, blocks, LANES)
    source_id = jnp.arange(sources, dtype=jnp.int32)
    needed = jnp.any((of_block[..., None] >> 7) == source_id, axis=(0, 2))
    block_id = jnp.arange(blocks, dtype=jnp.int32)
    before, after = (block_id - 1) % blocks, (block_id + 1) % blocks
    entries = jnp.moveaxis(of_block, 1, 0).reshape(blocks, 3 * LANES, 1)
    lane_id = jnp.arange(LANES, dtype=jnp.int32)

    def wanted(source):
        return jnp.any(entries == source[:, None, None] * LANES + lane_id, axis=1)

    want_before, want_after = wanted(before), wanted(after)
    merged = (
        jnp.any(want_before, axis=1)
        & jnp.any(want_after, axis=1)
        & ~jnp.any(want_before & want_after, axis=1)
    )
    second = merged[:, None] & (source_id == after[:, None])
    needed = needed & ~second
    rank = jnp.sum(
        needed[:, None, :] & (source_id[None, None, :] < source_id[None, :, None]), axis=2
    )
    place = jnp.where(
        second, jnp.sum(jnp.where(source_id == before[:, None], rank, 0), axis=1)[:, None], rank
    )
    listed = jnp.sum(
        jnp.where(
            needed[:, None, :] & (rank[:, None, :] == source_id[None, :, None]),
            source_id[None, None, :],
            0,
        ),
        axis=2,
    )
    also = jnp.where(merged[:, None] & (listed == before[:, None]), after[:, None], listed)
    place_of = jnp.sum(
        jnp.where((of_block[..., None] >> 7) == source_id, place[None, :, None, :], 0), axis=3
    )
    near_id = jnp.where(of_block < 0, -1, place_of * LANES + (of_block & (LANES - 1)))
    home = release_cell - lax.axis_index("region") * cells
    released = jnp.any(
        (home[None, :] >> 7) == jnp.arange(blocks, dtype=jnp.int32)[:, None], axis=1
    )
    plan = jnp.concatenate(
        [
            listed,
            also,
            jnp.broadcast_to(lax.axis_index("region") % 4, (blocks, 1)),
            jnp.sum(needed[:, :blocks], axis=1)[:, None],
            jnp.sum(needed, axis=1)[:, None],
            released[:, None],
        ],
        axis=1,
    ).astype(jnp.int32)
    near = jnp.concatenate(
        [
            jnp.broadcast_to(jnp.moveaxis(near_id, 1, 0)[:, :, None, :], (blocks, 3, 8, LANES)),
            jnp.broadcast_to(home[None, None, :, None], (blocks, 1, 8, LANES)),
            jnp.broadcast_to(want_before[:, None, None, :], (blocks, 1, 8, LANES)).astype(jnp.int32),
        ],
        axis=1,
    )
    near = kept(near)
    rate = kept(jnp.broadcast_to(release_rate[:, :, None], (layers, tracers, LANES)))

    coef_shape = (blocks, KINDS, layers, LANES)

    column = lax.axis_index("tracer")
    square = jnp.stack([column // 4, column % 4]).astype(jnp.int32)

    def prepare(table):
        return pl.pallas_call(
            prepare_kernel,
            out_shape=pltpu.HBM(coef_shape, f32),
            in_specs=[scalars] + [full] * len(table),
            out_specs=full,
            compiler_params=params(16),
            name="prepare",
        )(square, *table)

    tile = (layers, tracers, LANES)
    new_block = pltpu.HBM(tile, f32)
    halo_shape = pltpu.HBM((quads, *tile), f32)
    hbm = pl.BlockSpec(memory_space=pltpu.HBM)
    dma = pltpu.SemaphoreType.DMA

    def rim_step(field, received, coef, last):
        outs = (halo_shape, new_block) if last else (message, halo_shape, new_block)
        vmem = pltpu.VMEM
        scratch = [
            vmem((2 * blocks, *tile), f32),
            vmem(tile, f32),
            vmem((1, *coef_shape[1:]), f32),
            vmem((1, 5, 8, LANES), jnp.int32),
            vmem(tile, f32),
            vmem(halo_shape.shape, f32),
            vmem(tile, f32),
            vmem((1, *tile), f32),
        ]
        scratch += [] if last else [vmem(message.shape, f32)]
        scratch += [dma((4,)), dma((2 * blocks,)), dma((2 + quads,))]
        result = pl.pallas_call(
            functools.partial(rim_kernel, last),
            out_shape=outs,
            in_specs=[scalars, hbm, full, hbm, hbm, hbm] + ([] if last else [full]),
            out_specs=(hbm,) * len(outs),
            scratch_shapes=scratch,
            compiler_params=params(20),
            name="rim",
        )(plan, kept(field), received, kept(coef), near, rate, *(() if last else (lanes,)))
        return result if not last else (None, *result)

    def bulk_step(field, halo, new, coef, early):
        vmem = pltpu.VMEM
        return pl.pallas_call(
            bulk_kernel,
            out_shape=pltpu.HBM(field.shape, f32),
            in_specs=[scalars] + [hbm] * 7,
            out_specs=hbm,
            scratch_shapes=[
                vmem(field.shape, f32),
                vmem(halo_shape.shape, f32),
                vmem(coef_shape, f32),
                vmem((blocks, 5, 8, LANES), jnp.int32),
                vmem(tile, f32),
                vmem((GROUP, *tile), f32),
                vmem(field.shape, f32),
                dma((4 + (blocks - 1) // GROUP,)),
                dma((1 + (blocks - 1) // GROUP,)),
            ],
            compiler_params=params(24),
            name="bulk",
        )(plan, kept(field), kept(halo), kept(new), kept(coef), near, rate, kept(early))

    part_shape = pltpu.HBM((blocks, *tile), f32)

    def last_step_local(field, coef):
        vmem = pltpu.VMEM
        return pl.pallas_call(
            local_kernel,
            out_shape=part_shape,
            in_specs=[scalars] + [hbm] * 4,
            out_specs=hbm,
            scratch_shapes=[
                vmem(field.shape, f32),
                vmem(coef_shape, f32),
                vmem((blocks, 5, 8, LANES), jnp.int32),
                vmem(tile, f32),
                vmem(part_shape.shape, f32),
                dma((4,)),
                dma((blocks,)),
            ],
            compiler_params=params(24),
            name="local",
        )(plan, kept(field), kept(coef), near, rate)

    def last_step(part, received, coef):
        vmem = pltpu.VMEM
        return pl.pallas_call(
            finish_kernel,
            out_shape=pltpu.HBM(concentration.shape, f32),
            in_specs=[scalars, hbm, full, hbm, hbm],
            out_specs=hbm,
            scratch_shapes=[
                vmem(part_shape.shape, f32),
                vmem(coef_shape, f32),
                vmem((blocks, 5, 8, LANES), jnp.int32),
                vmem(halo_shape.shape, f32),
                vmem(concentration.shape, f32),
                dma((1 + 2 * (blocks // 4),)),
                dma((blocks // 4,)),
            ],
            compiler_params=params(24),
            name="finish",
        )(plan, kept(part), received, kept(coef), near)

    field = concentration
    per_hour = STEPS // HOURS
    coef = prepare(share(panel(0)))
    for step in range(STEPS - 1):
        early = rate
        send, halo, new = rim_step(field, received, coef, False)
        received = lax.all_to_all(send, "region", 0, 0, tiled=True)
        if step == 0:
            later, _ = lax.optimization_barrier((panel(1), new))
            row_panels = share_side(later, 0)
        if step == 1:
            panels = share_side(row_panels, 1)
        if step == per_hour - 1:
            early = later_coef = prepare((panels,))
        field = bulk_step(field, halo, new, coef, early)
        if step == per_hour - 1:
            coef = later_coef
    part = last_step_local(field, coef)
    return last_step(part, received, coef)


def solution(mesh):
    both = ("region", "tracer")
    return jax.shard_map(
        transport,
        mesh=mesh,
        in_specs=(
            P(None, "tracer", "region"),
            P(None, None, None, both),
            P(None, None, both),
            P(None, "tracer"),
            P("tracer"),
            P(None, "region"),
            P("region", None, None),
        ),
        out_specs=P(None, "tracer", "region"),
        check_vma=False,
    )
```
